512 devices in a mesh: phi: 64 (over z, y_hi, core), row: 8 (over y_lo, x).
Axes of the slice: x: 4, y: 4 (y_hi: 2, y_lo: 2; y = y_hi * 2 + y_lo), z: 16, core: 2. Of those that a mesh axis runs over, the one named last changes fastest.
Arguments:
- density: float32 [3, 2, 4096, 1024], P(None, None, 'phi', 'row'), may hold values from 0.5 to 2
- phi_speed: float32 [3, 2, 4096, 1024], P(None, None, 'phi', 'row'), may hold values from -0.3 to 0.3
- rad_speed: float32 [3, 2, 4096, 1024], P(None, None, 'phi', 'row'), may hold values from -0.3 to 0.3
- profile: float32 [2], replicated, may hold values from 0.2 to 1
- tiles: float32 [2, 4096, 8, 1024], P(None, 'phi', None, 'row'), may hold values from -3 to 3
- owners: int32 [2, 4096, 1], P(None, 'phi'), may hold values from 0 to 63; in each aligned block of 64 rows (0 to 63, 64 to 127, ..., all dimensions but the last counted through in order) at most 2 rows name the same one
- slots: int32 [2, 4096], P(None, 'phi'), may hold values from 0 to 7
- shifts: int32 [2, 1024], P(None, 'row'), may hold values from 0 to 4095
Outputs:
- advanced: float32 [3, 2, 4096, 1024], P(None, None, 'phi', 'row')
The draws below stay inside these ranges and needn't reach their ends.
Inputs may be any that keep to these rules, and one draw needn't show every extreme that they name: `owners`: in each step, among the 64 tiles held by one index of phi, at most 2 name the same owner.
All inputs are finite; a program needn't handle non-finite values.
Results may differ from the reference program's by a relative error of at most 0.000086.
Values sent between devices are 32-bit elements; how exact they have to be, the bound alone decides.
A program may use at most 128 MiB of HBM per device.

```python
import math
import jax
import jax.numpy as jnp
import numpy as np
from jax import lax

FLUIDS = 3
LAYERS = 2
PHI_DEV = 64
STEPS = 2
TILE_PHI = 8
CAP = 2
NPHI = 4096
NR = 1024
TILES_DEV = 64
TILES = 4096
SLOTS = 8
N_PHI = 64


def place_ends(result, stream_key, low, top_value):
    spot = [jax.random.randint(jax.random.fold_in(stream_key, axis), (), 0, length) for axis, length in enumerate(result.shape)]
    main_axis = result.shape.index(max(result.shape))
    next_to = spot[:main_axis] + [(spot[main_axis] + 1) % result.shape[main_axis]] + spot[main_axis + 1:]
    return result.at[tuple(spot)].set(low).at[tuple(next_to)].set(top_value)


def block_scale(rng, extent, cuts, smallest, high):
    def one(axis_at, shards_of):
        heights = jax.random.uniform(jax.random.fold_in(jax.random.fold_in(rng, 6), axis_at), (shards_of,), jnp.float32, smallest / len(cuts), high / len(cuts))
        return jnp.repeat(jnp.exp(heights), extent[axis_at] // shards_of).reshape((-1,) + (1,) * (len(extent) - axis_at - 1))

    loudness = one(*cuts[0])
    for cut in cuts[1:]:
        loudness = loudness * one(*cut)
    return loudness


def routed_block(key, own, number, rows, number_of, top, reach, lean):
    order = jax.random.permutation(key, number_of)
    heavy_load, usual = shares(number_of, rows * top, reach, lean, True), shares(number_of, rows * top, reach, lean, False)
    places = jnp.arange(number_of)

    def named(tallies, rotation):
        used = int((tallies > 0).sum())
        fixed = max(1, used // 4)
        moved = fixed + (places - fixed + rotation * (used - fixed)) % max(1, number_of - fixed)
        return jnp.zeros((number_of,), jnp.int32).at[order[jnp.where(places < fixed, places, moved)]].set(jnp.asarray(tallies, jnp.int32))

    tallies = jnp.where(number % 4 == 0, named(heavy_load, number // 4), named(usual, number - number // 4 - 1))
    mixed = jax.random.permutation(jax.random.fold_in(own, 3), number_of)
    donor, sink = mixed[0:number_of // 2 * 2:2], mixed[1:number_of // 2 * 2:2]
    room = jnp.minimum(tallies[donor] - 1, reach - tallies[sink]) // 2
    room = jnp.where((donor == order[0]) | (sink == order[0]) | (tallies[sink] == 0), 0, jnp.maximum(room, 0))
    moved = jax.random.randint(jax.random.fold_in(own, 4), (number_of // 2,), 0, 1 << 20) % (room + 1)
    tallies = tallies.at[donor].add(-moved).at[sink].add(moved)
    members = jnp.searchsorted(jnp.cumsum(tallies), jnp.arange(rows * top), side="right").astype(jnp.int32)
    table = members.reshape(top, rows).T
    table = table[jax.random.permutation(jax.random.fold_in(own, 1), rows)]
    rotation = jax.random.randint(jax.random.fold_in(own, 2), (rows, 1), 0, top)
    return jnp.take_along_axis(table, (jnp.arange(top)[None, :] + rotation) % top, axis=1)


def shares(count, total, most, skew, full):
    loads = [(1 << 20) // math.isqrt(rank ** skew) + 1 for rank in range(1, count + 1)]
    largest = most if full else min(most, max(-(-total // count), total * loads[0] // sum(loads)))
    least = 1 if total - largest >= count - 1 else 0
    counts, spare = [largest] + [least] * (count - 1), total - largest - least * (count - 1)
    while spare > 0:
        movable = [i for i in range(1, count) if counts[i] < largest] or [i for i in range(1, count) if counts[i] < most]
        whole, remaining = sum([loads[i] for i in movable]), spare
        for i in movable:
            addition = min(most - counts[i], max(1, remaining * loads[i] // whole), spare)
            counts[i] = counts[i] + addition
            spare = spare - addition
    return np.array(counts)


def noise(key, shape, width, reach, pieces=(), held_as=jnp.bfloat16):
    gain = block_scale(key, shape, pieces, -0.22, 0.18) if pieces else 1.0
    array = jax.random.normal(key, shape, jnp.float32) * width * gain
    return jnp.minimum(jnp.maximum(array, -reach), reach).astype(held_as)


def setup_inputs(seed: int = 0) -> dict:
    key_list = jax.random.split(jax.random.key(seed), 9)
    density = jnp.clip(jnp.exp(math.log(2.0) - 1.3862944 * jax.random.uniform(key_list[0], (FLUIDS, LAYERS, NPHI, NR), jnp.float32) ** block_scale(key_list[0], (FLUIDS, LAYERS, NPHI, NR), ((2, 64), (3, 8)), -0.2, 0.2)), 0.5, 2.0)
    phi_speed = jnp.clip(jax.random.uniform(key_list[1], (FLUIDS, LAYERS, NPHI, NR), jnp.float32, -0.3, 0.3) * block_scale(key_list[1], (FLUIDS, LAYERS, NPHI, NR), ((2, 64), (3, 8)), -0.4, 0.0), -0.3, 0.3)
    rad_speed = jnp.clip(jax.random.uniform(key_list[2], (FLUIDS, LAYERS, NPHI, NR), jnp.float32, -0.3, 0.3) * block_scale(key_list[2], (FLUIDS, LAYERS, NPHI, NR), ((2, 64), (3, 8)), -0.4, 0.0), -0.3, 0.3)
    profile = jnp.clip(jnp.exp(jax.random.uniform(key_list[3], (LAYERS,), jnp.float32, math.log(0.2), math.log(1.0))), 0.2, 1.0)
    tiles = noise(key_list[4], (STEPS, TILES, TILE_PHI, NR), 0.5, 3.0, ((1, 64), (3, 8)), jnp.float32)
    owners_keys = jax.random.split(jax.random.fold_in(key_list[5], 1), STEPS * TILES // TILES_DEV)
    owners_turns = jax.random.permutation(jax.random.fold_in(key_list[5], 3), STEPS * TILES // TILES_DEV)
    owners = jax.vmap(lambda own, number: routed_block(jax.random.fold_in(key_list[5], 2), own, number, TILES_DEV, N_PHI, 1, CAP, 2))(owners_keys, owners_turns).reshape((STEPS, TILES, 1))
    slots = place_ends(jax.random.randint(key_list[6], (STEPS, TILES), 0, SLOTS), jax.random.fold_in(key_list[6], 1), 0, SLOTS - 1).astype(jnp.int32)
    shifts = place_ends(jax.random.randint(key_list[7], (STEPS, NR), 0, NPHI), jax.random.fold_in(key_list[7], 1), 0, NPHI - 1).astype(jnp.int32)
    return {"density": density, "phi_speed": phi_speed, "rad_speed": rad_speed, "profile": profile, "tiles": tiles, "owners": owners, "slots": slots, "shifts": shifts}


def update(mass, behind, ahead_cells, speed_phi, speed_next, inner_cells, outer_cells, speed_rad, radial_next):
    flux_in = jnp.maximum(speed_phi, 0.0) * behind + jnp.minimum(speed_phi, 0.0) * mass
    flux_out = jnp.maximum(speed_next, 0.0) * mass + jnp.minimum(speed_next, 0.0) * ahead_cells
    radial_in = jnp.maximum(speed_rad, 0.0) * inner_cells + jnp.minimum(speed_rad, 0.0) * mass
    radial_out = jnp.maximum(radial_next, 0.0) * mass + jnp.minimum(radial_next, 0.0) * outer_cells
    return mass - (flux_out - flux_in) - (radial_out - radial_in)


def transport_one(fields):
    mass, speed_phi, speed_rad = fields
    behind = jnp.roll(mass, 1, 1)
    ahead_cells = jnp.roll(mass, -1, 1)
    speed_next = jnp.roll(speed_phi, -1, 1)
    inner_cells = jnp.pad(mass, ((0, 0), (0, 0), (1, 0)))[:, :, :-1]
    outer_cells = jnp.pad(mass, ((0, 0), (0, 0), (0, 1)))[:, :, 1:]
    radial_next = jnp.pad(speed_rad, ((0, 0), (0, 0), (0, 1)))[:, :, 1:]
    return update(mass, behind, ahead_cells, speed_phi, speed_next, inner_cells, outer_cells, speed_rad, radial_next)


def reference(density, phi_speed, rad_speed, profile, tiles, owners, slots, shifts):
    mass = density
    for number in range(STEPS):
        mass = lax.map(transport_one, (mass, phi_speed, rad_speed))
        positions = (owners[number, :, 0] * PHI_DEV + slots[number] * TILE_PHI)[:, None] + jnp.arange(TILE_PHI, dtype=jnp.int32)[None, :]
        deposit = jnp.zeros((NPHI, NR), jnp.float32).at[positions.reshape(-1)].add(tiles[number].reshape(-1, NR))
        mass = mass.at[0].add(profile[:, None, None] * deposit[None])
        source_index = (jnp.arange(NPHI, dtype=jnp.int32)[:, None] - shifts[number][None, :]) % NPHI

        def roll_plane(plane):
            return jnp.take_along_axis(plane, source_index, 0)

        mass = jax.vmap(roll_plane)(mass.reshape(FLUIDS * LAYERS, NPHI, NR)).reshape(mass.shape)
    return mass
```

```python
import jax
import jax.numpy as jnp
from jax import lax
from jax.experimental import pallas as pl
from jax.experimental.pallas import tpu as pltpu
from jax.sharding import PartitionSpec as P


def rims(field, axis, dim, closed):
    count = lax.axis_size(axis)
    ends = count if closed else count - 1
    size = field.shape[dim]
    head = lax.slice_in_dim(field, 0, 1, axis=dim)
    tail = lax.slice_in_dim(field, size - 1, size, axis=dim)
    before = lax.ppermute(tail, axis, [(i, (i + 1) % count) for i in range(ends)])
    after = lax.ppermute(head, axis, [((i + 1) % count, i) for i in range(ends)])
    return before, after


def after_rim(field, axis, dim, closed):
    count = lax.axis_size(axis)
    ends = count if closed else count - 1
    head = lax.slice_in_dim(field, 0, 1, axis=dim)
    return lax.ppermute(head, axis, [((i + 1) % count, i) for i in range(ends)])


def update(mass, behind, ahead, speed_phi, speed_next, inner, outer, speed_rad, radial_next):
    flux_in = jnp.maximum(speed_phi, 0.0) * behind + jnp.minimum(speed_phi, 0.0) * mass
    flux_out = jnp.maximum(speed_next, 0.0) * mass + jnp.minimum(speed_next, 0.0) * ahead
    radial_in = jnp.maximum(speed_rad, 0.0) * inner + jnp.minimum(speed_rad, 0.0) * mass
    radial_out = jnp.maximum(radial_next, 0.0) * mass + jnp.minimum(radial_next, 0.0) * outer
    return mass - (flux_out - flux_in) - (radial_out - radial_in)


def exchange(chunks):
    return lax.all_to_all(chunks, "phi", split_axis=0, concat_axis=0, tiled=True)


def pack(planes, count):
    rows, cells, width = planes.shape
    per = width // count
    return planes.reshape(rows, cells, per, count).transpose(3, 0, 2, 1).reshape(count, rows, per * cells)


def unpack(chunks, width):
    count, rows, lanes = chunks.shape
    per = width // count
    cells = lanes // per
    return chunks.reshape(count, rows, per, cells).transpose(1, 3, 2, 0).reshape(rows, cells, width)


def shift_kernel(whole_ref, chunk_ref, extra_ref, rest_ref, out_ref, twice):
    count, rows, lanes = out_ref.shape
    half = lanes // 2
    chunk = chunk_ref[:, :rows, :] + extra_ref[...]
    twice[pl.ds(1, count)] = chunk
    twice[pl.ds(1 + count, count)] = chunk
    twice[0] = chunk[count - 1]
    lane = lax.broadcasted_iota(jnp.int32, (1, 1, lanes), 2)
    rest = rest_ref[...].reshape(1, 1, lanes)
    first = lane < half
    low, high = whole_ref[0], whole_ref[1]
    here = jnp.where(first, twice[pl.ds(1 + count - low, count)], twice[pl.ds(1 + count - high, count)])
    prev = jnp.where(first, twice[pl.ds(count - low, count)], twice[pl.ds(count - high, count)])
    inside = lane % half
    mixed = jnp.where(inside < half - rest, here, prev)
    source = (lane - inside) + (inside - rest) % half
    index = jnp.broadcast_to(source, mixed.shape).reshape(count * rows, lanes)
    out_ref[...] = jnp.take_along_axis(mixed.reshape(count * rows, lanes), index, axis=1).reshape(mixed.shape)


def shifted(chunk, extra, whole, rest):
    count, rows, lanes = extra.shape
    return pl.pallas_call(
        shift_kernel,
        out_shape=jax.ShapeDtypeStruct((count, rows, lanes), jnp.float32),
        in_specs=[pl.BlockSpec(memory_space=pltpu.SMEM)] + [pl.BlockSpec(memory_space=pltpu.VMEM)] * 3,
        out_specs=pl.BlockSpec(memory_space=pltpu.VMEM),
        scratch_shapes=[pltpu.VMEM((2 * count + 1, rows, lanes), jnp.float32)],
    )(whole, chunk, extra, rest)


def body(density, phi_speed, rad_speed, profile, tiles, owners, slots, shifts):
    fluids, layers, cells, width = density.shape
    planes = fluids * layers
    count = lax.axis_size("phi")
    per = width // count
    steps, held, strip = tiles.shape[:3]
    places = cells // strip
    me = lax.axis_index("phi")
    shape = (planes, cells, width)
    mass, speed_phi, speed_rad = (a.reshape(shape) for a in (density, phi_speed, rad_speed))
    speed_next = jnp.concatenate([speed_phi[:, 1:], after_rim(speed_phi, "phi", 1, True)], 1)
    radial_next = jnp.concatenate([speed_rad[:, :, 1:], after_rim(speed_rad, "row", 2, False)], 2)

    packed_tiles = (
        tiles.reshape(steps, held, strip, per, count).transpose(4, 0, 2, 3, 1).reshape(count, steps * strip, per * held)
    )
    strips = exchange(packed_tiles).reshape(count, steps, strip, per, held)
    labels = (owners[:, :, 0] * places + slots).astype(jnp.float32).reshape(1, 1, steps * held)
    labels = jnp.broadcast_to(labels, (count, 1, steps * held))
    targets = jnp.arange(count * places, dtype=jnp.int32)
    for number in range(steps):
        behind, ahead = rims(mass, "phi", 1, True)
        inner, outer = rims(mass, "row", 2, False)
        mass = update(
            mass,
            jnp.concatenate([behind, mass[:, :-1]], 1),
            jnp.concatenate([mass[:, 1:], ahead], 1),
            speed_phi,
            speed_next,
            jnp.concatenate([inner, mass[:, :, :-1]], 2),
            jnp.concatenate([mass[:, :, 1:], outer], 2),
            speed_rad,
            radial_next,
        )
        chunk = pack(mass, count)
        if number == 0:
            chunk = exchange(jnp.concatenate([chunk, labels], 1))
            known = chunk[:, planes, :].astype(jnp.int32).reshape(count, steps, held)
        else:
            chunk = exchange(chunk)
        onehot = (known[:, number].reshape(-1)[:, None] == targets[None, :]).astype(jnp.bfloat16)
        values = strips[:, number].transpose(2, 1, 0, 3).reshape(per * strip, count * held)
        high = lax.reduce_precision(values, 8, 7)
        middle = lax.reduce_precision(values - high, 8, 7)
        parts = jnp.concatenate([high, middle, values - high - middle], 0).astype(jnp.bfloat16)
        sums = jnp.dot(parts, onehot, preferred_element_type=jnp.float32)
        sums = sums.reshape(3, per, strip, count, places).sum(0)
        deposit = sums.transpose(2, 0, 3, 1).reshape(count, 1, per * cells)
        weight = jnp.concatenate([profile, jnp.zeros((planes - layers,), jnp.float32)])
        extra = deposit * weight[None, :, None]
        mine = shifts[number].reshape(per, count)
        mine = lax.dynamic_slice_in_dim(mine, me, 1, axis=1)[:, 0]
        rest = jnp.repeat(mine % cells, cells).reshape(1, per * cells)
        chunk = shifted(chunk, extra, mine // cells, rest)
        mass = unpack(exchange(chunk), width)
    return mass.reshape(density.shape)


def solution(mesh):
    placed = (
        P(None, None, "phi", "row"),
        P(None, None, "phi", "row"),
        P(None, None, "phi", "row"),
        P(),
        P(None, "phi", None, "row"),
        P(None, "phi", None),
        P(None, "phi"),
        P(None, "row"),
    )
    return jax.shard_map(
        body, mesh=mesh, in_specs=placed, out_specs=P(None, None, "phi", "row"), check_vma=False
    )
```

```python
import jax
import jax.numpy as jnp
from jax import lax
from jax.experimental import pallas as pl
from jax.experimental.pallas import tpu as pltpu
from jax.sharding import PartitionSpec as P

MESH = pl.DeviceIdType.MESH


def fold(block):
    turned = block.T
    count = turned.shape[0] // 2
    return jnp.concatenate([turned[:count], turned[count:]], axis=1)


def unfold(block):
    half = block.shape[1] // 2
    return jnp.concatenate([block[:, :half], block[:, half:]], axis=0).T


def fused(
    whole_ref,
    profile_ref,
    rest_ref,
    names_ref,
    mass_ref,
    phi_ref,
    rad_ref,
    tiles_ref,
    out_ref,
    edge_out,
    edge_in,
    names_in,
    tile_out,
    tile_in,
    mass_out,
    mass_in,
    twice,
    held_mass,
    lhs,
    rhs,
    deposit,
    edge_send,
    edge_recv,
    all_send,
    all_recv,
):
    planes, cells, width = mass_ref.shape
    steps = tiles_ref.shape[0]
    strip = tiles_ref.shape[2]
    places = cells // strip
    count, row_count = lax.axis_size("phi"), lax.axis_size("row")
    me, row = lax.axis_index("phi"), lax.axis_index("row")
    lanes = 2 * cells
    up, down = lax.rem(me + 1, count), lax.rem(me + count - 1, count)
    outward, inward = lax.rem(row + 1, row_count), lax.rem(row + row_count - 1, row_count)

    barrier = pltpu.get_barrier_semaphore()

    @pl.loop(1, count)
    def _(step):
        pl.semaphore_signal(barrier, inc=1, device_id={"phi": lax.rem(me + step, count)}, device_id_type=MESH)

    pl.semaphore_signal(barrier, inc=1, device_id={"row": outward}, device_id_type=MESH)
    pl.semaphore_signal(barrier, inc=1, device_id={"row": inward}, device_id_type=MESH)

    def put_column(place, field, column):
        rows = [field[f].T[column : column + 1, :] for f in range(planes)]
        edge_out[place, :planes, :cells] = jnp.concatenate(rows, axis=0)

    def put_row(place, field, at):
        edge_out[place, :planes, :width] = field[:, at, :]

    def edge(place, target):
        return pltpu.make_async_remote_copy(
            src_ref=edge_out.at[place],
            dst_ref=edge_in.at[place],
            send_sem=edge_send.at[place],
            recv_sem=edge_recv.at[place],
            device_id=target,
            device_id_type=MESH,
        )

    def mass_edges(base, field):
        put_row(base, field, cells - 1)
        put_row(base + 1, field, 0)
        put_column(base + 2, field, width - 1)
        put_column(base + 3, field, 0)
        return [
            edge(base, {"phi": up}),
            edge(base + 1, {"phi": down}),
            edge(base + 2, {"row": outward}),
            edge(base + 3, {"row": inward}),
        ]

    def send_all(source, target, number):
        @pl.loop(1, count)
        def _(step):
            peer = lax.rem(me + step, count)
            pltpu.make_async_remote_copy(
                src_ref=source.at[peer],
                dst_ref=target.at[me],
                send_sem=all_send.at[number],
                recv_sem=all_recv.at[number],
                device_id={"phi": peer},
                device_id_type=MESH,
            ).start()

        target[pl.ds(me, 1)] = source[pl.ds(me, 1)]

    def all_wait(target, semaphore):
        others = target.at[pl.ds(0, count - 1)]
        pltpu.make_async_copy(others, others, semaphore).wait()

    density = mass_ref[...]
    first_edges = mass_edges(0, density)
    put_row(8, phi_ref, 0)
    put_column(9, rad_ref, 0)
    first_edges += [edge(8, {"phi": down}), edge(9, {"row": inward})]
    names_in[pl.ds(me, 1)] = names_ref[...]

    pl.semaphore_wait(barrier, count + 1)
    for copy in first_edges:
        copy.start()

    @pl.loop(1, count)
    def _(step):
        pltpu.make_async_remote_copy(
            src_ref=names_ref.at[0],
            dst_ref=names_in.at[me],
            send_sem=all_send.at[0],
            recv_sem=all_recv.at[0],
            device_id={"phi": lax.rem(me + step, count)},
            device_id_type=MESH,
        ).start()

    def send_tiles(number):
        for p in range(strip):
            tile_out[number, :, p, :] = fold(tiles_ref[number, :, p, :])
        send_all(tile_out.at[number], tile_in.at[number], 1 + number)

    send_tiles(0)

    lane = lax.broadcasted_iota(jnp.int32, (1, 1, width), 2)
    cell = lax.broadcasted_iota(jnp.int32, (1, cells, 1), 1)

    def rows_of(place):
        return edge_in[place, :planes, :width].reshape(planes, 1, width)

    def columns_of(place, outside):
        turned = edge_in[place].T
        found = jnp.stack([turned[:cells, f : f + 1] for f in range(planes)], axis=0)
        return jnp.where(outside, 0.0, found)

    for copy in first_edges:
        copy.wait()
    speed_phi, speed_rad = phi_ref[...], rad_ref[...]
    speed_next = jnp.where(cell == cells - 1, rows_of(8), pltpu.roll(speed_phi, cells - 1, 1))
    last_row = row == row_count - 1
    radial_next = jnp.where(lane == width - 1, columns_of(9, last_row), pltpu.roll(speed_rad, width - 1, 2))

    def advance(mass, base):
        behind = jnp.where(cell == 0, rows_of(base), pltpu.roll(mass, 1, 1))
        ahead = jnp.where(cell == cells - 1, rows_of(base + 1), pltpu.roll(mass, cells - 1, 1))
        inner = jnp.where(lane == 0, columns_of(base + 2, row == 0), pltpu.roll(mass, 1, 2))
        outer = jnp.where(lane == width - 1, columns_of(base + 3, last_row), pltpu.roll(mass, width - 1, 2))
        flux_in = jnp.maximum(speed_phi, 0.0) * behind + jnp.minimum(speed_phi, 0.0) * mass
        flux_out = jnp.maximum(speed_next, 0.0) * mass + jnp.minimum(speed_next, 0.0) * ahead
        radial_in = jnp.maximum(speed_rad, 0.0) * inner + jnp.minimum(speed_rad, 0.0) * mass
        radial_out = jnp.maximum(radial_next, 0.0) * mass + jnp.minimum(radial_next, 0.0) * outer
        return mass - (flux_out - flux_in) - (radial_out - radial_in)

    def send_mass(mass, turn, number):
        for f in range(planes):
            mass_out[turn, :, f, :] = fold(mass[f])
        send_all(mass_out.at[turn], mass_in.at[turn], number)

    def make_deposit(number):
        line = lax.broadcasted_iota(jnp.int32, (lanes, lanes), 0)
        spot = lax.broadcasted_iota(jnp.int32, (lanes, lanes), 1)
        same = (line >= cells) == (spot >= cells)
        owner_line = lax.rem(line, cells).astype(jnp.float32)

        deposit[...] = jnp.zeros_like(deposit)

        @pl.loop(0, count // 2)
        def _(pair):
            for side in range(2):
                source = 2 * pair + side
                names = names_in[source]
                own, slot = names[2 * number : 2 * number + 1], names[2 * number + 1 : 2 * number + 2]
                block = tile_in[number, source]
                high = block.astype(jnp.bfloat16).astype(jnp.float32)
                left = block - high
                middle = left.astype(jnp.bfloat16).astype(jnp.float32)
                low = left - middle
                span = slice(side * lanes, (side + 1) * lanes)
                for n, part in enumerate((high, middle, low)):
                    spread = [jnp.where(slot == float(q), part, 0.0) for q in range(places)]
                    rhs[n * cells : (n + 1) * cells, span] = jnp.concatenate(spread, axis=0).astype(jnp.bfloat16)
                hit = jnp.where(same & (own == owner_line), 1.0, 0.0)
                lhs[:, span] = hit.astype(jnp.bfloat16)
            deposit[...] += lax.dot_general(
                lhs[...], rhs[...], (((1,), (1,)), ((), ())), preferred_element_type=jnp.float32
            )

        total = deposit[:, :cells] + deposit[:, cells : 2 * cells] + deposit[:, 2 * cells : 3 * cells]
        return jnp.concatenate([total[:count], total[cells : cells + count]], axis=1)

    spot = lax.broadcasted_iota(jnp.int32, (1, 1, lanes), 2)
    inside = lax.rem(spot, cells)

    def turn_back(source, number, added, turn, channel):
        for f in range(planes):
            block = source[:, f, :]
            if f < profile_ref.shape[0]:
                block = block + profile_ref[f] * added
            twice[pl.ds(1, count), f, :] = block
            twice[pl.ds(1 + count, count), f, :] = block
            twice[0, f : f + 1, :] = block[count - 1 :]
        rest = rest_ref[number : number + 1].reshape(1, 1, lanes)
        low, high = whole_ref[number, 0], whole_ref[number, 1]
        here = jnp.where(spot < cells, twice[pl.ds(1 + count - low, count)], twice[pl.ds(1 + count - high, count)])
        prev = jnp.where(spot < cells, twice[pl.ds(count - low, count)], twice[pl.ds(count - high, count)])
        mixed = jnp.where(inside < cells - rest, here, prev)
        moved = inside - rest
        index = (spot - inside) + jnp.where(moved < 0, moved + cells, moved)
        index = jnp.broadcast_to(index, mixed.shape).reshape(count * planes, lanes)
        mass_out[turn] = jnp.take_along_axis(mixed.reshape(count * planes, lanes), index, axis=1).reshape(mixed.shape)
        send_all(mass_out.at[turn], mass_in.at[turn], channel)

    send_mass(advance(density, 0), 0, 3)
    send_tiles(1)
    all_wait(names_in, all_recv.at[0])
    all_wait(tile_in.at[0], all_recv.at[1])
    added = make_deposit(0)
    all_wait(mass_in.at[0], all_recv.at[3])
    turn_back(mass_in.at[0], 0, added, 1, 4)
    all_wait(tile_in.at[1], all_recv.at[2])
    added = make_deposit(1)
    all_wait(mass_in.at[1], all_recv.at[4])
    for f in range(planes):
        held_mass[f] = unfold(mass_in[1, :, f, :])
    mass = held_mass[...]
    second_edges = mass_edges(4, mass)
    for copy in second_edges:
        copy.start()
    for copy in second_edges:
        copy.wait()
    send_mass(advance(mass, 4), 2, 5)
    all_wait(mass_in.at[2], all_recv.at[5])
    turn_back(mass_in.at[2], 1, added, 3, 6)
    all_wait(mass_in.at[3], all_recv.at[6])
    for f in range(planes):
        out_ref[f] = unfold(mass_in[3, :, f, :])
    all_wait(names_in, all_send.at[0])
    for number in range(steps):
        all_wait(tile_out.at[number], all_send.at[1 + number])
    for turn in range(4):
        all_wait(mass_out.at[turn], all_send.at[3 + turn])


def body(density, phi_speed, rad_speed, profile, tiles, owners, slots, shifts):
    fluids, layers, cells, width = density.shape
    planes = fluids * layers
    count = lax.axis_size("phi")
    per = width // count
    steps, held, strip = tiles.shape[:3]
    lanes = per * cells
    me = lax.axis_index("phi")
    shape = (planes, cells, width)
    mine = lax.dynamic_slice_in_dim(shifts.reshape(steps, per, count), me, 1, axis=2)[:, :, 0]
    whole = mine // cells
    rest = jnp.repeat(mine % cells, cells, axis=1)
    names = jnp.stack([owners[:, :, 0], slots], axis=1).astype(jnp.float32)
    names = jnp.tile(names, (1, 1, per)).reshape(1, 2 * steps, lanes)
    smem, vmem = pl.BlockSpec(memory_space=pltpu.SMEM), pl.BlockSpec(memory_space=pltpu.VMEM)
    sent = 4 * count * lanes * (4 * planes + 2 * strip + 4)
    out = pl.pallas_call(
        fused,
        out_shape=jax.ShapeDtypeStruct(shape, jnp.float32),
        in_specs=[smem] * 2 + [vmem] * 6,
        out_specs=vmem,
        scratch_shapes=[
            pltpu.VMEM((10, 8, 128), jnp.float32),
            pltpu.VMEM((10, 8, 128), jnp.float32),
            pltpu.VMEM((count, 2 * steps, lanes), jnp.float32),
            pltpu.VMEM((steps, count, strip, lanes), jnp.float32),
            pltpu.VMEM((steps, count, strip, lanes), jnp.float32),
            pltpu.VMEM((4, count, planes, lanes), jnp.float32),
            pltpu.VMEM((4, count, planes, lanes), jnp.float32),
            pltpu.VMEM((2 * count + 1, planes, lanes), jnp.float32),
            pltpu.VMEM(shape, jnp.float32),
            pltpu.VMEM((lanes, 2 * lanes), jnp.bfloat16),
            pltpu.VMEM((3 * cells, 2 * lanes), jnp.bfloat16),
            pltpu.VMEM((lanes, 3 * cells), jnp.float32),
            pltpu.SemaphoreType.DMA((10,)),
            pltpu.SemaphoreType.DMA((10,)),
            pltpu.SemaphoreType.DMA((7,)),
            pltpu.SemaphoreType.DMA((7,)),
        ],
        compiler_params=pltpu.CompilerParams(
            collective_id=0, has_side_effects=True, vmem_limit_bytes=48 * 1024 * 1024
        ),
        cost_estimate=pl.CostEstimate(flops=10**9, bytes_accessed=sent, transcendentals=0),
    )(
        whole,
        profile,
        rest,
        names,
        density.reshape(shape),
        phi_speed.reshape(shape),
        rad_speed.reshape(shape),
        tiles,
    )
    return out.reshape(density.shape)


def solution(mesh):
    placed = (
        P(None, None, "phi", "row"),
        P(None, None, "phi", "row"),
        P(None, None, "phi", "row"),
        P(),
        P(None, "phi", None, "row"),
        P(None, "phi", None),
        P(None, "phi"),
        P(None, "row"),
    )
    return jax.shard_map(
        body, mesh=mesh, in_specs=placed, out_specs=P(None, None, "phi", "row"), check_vma=False
    )
```

```python
import jax
import jax.numpy as jnp
from jax import lax
from jax.experimental import pallas as pl
from jax.experimental.pallas import tpu as pltpu
from jax.sharding import PartitionSpec as P

MESH = pl.DeviceIdType.MESH


def fold(block):
    turned = block.T
    count = turned.shape[0] // 2
    return jnp.concatenate([turned[:count], turned[count:]], axis=1)


def unfold(block):
    half = block.shape[1] // 2
    return jnp.concatenate([block[:, :half], block[:, half:]], axis=0).T


def fused(
    whole_ref,
    profile_ref,
    rest_ref,
    names_ref,
    mass_hbm,
    phi_hbm,
    rad_hbm,
    tiles_hbm,
    out_ref,
    mass_ref,
    phi_ref,
    rad_ref,
    tiles_ref,
    edge_out,
    edge_in,
    names_in,
    tile_out,
    tile_in,
    gas_out,
    gas_in,
    gas_twice,
    dust_out,
    dust_in,
    dust_twice,
    held_mass,
    lhs,
    rhs,
    deposit,
    edge_send,
    edge_recv,
    all_send,
    all_recv,
    load,
):
    planes, cells, width = mass_ref.shape
    steps = tiles_ref.shape[0]
    strip = tiles_ref.shape[2]
    places = cells // strip
    count, row_count = lax.axis_size("phi"), lax.axis_size("row")
    me, row = lax.axis_index("phi"), lax.axis_index("row")
    lanes = 2 * cells
    up, down = lax.rem(me + 1, count), lax.rem(me + count - 1, count)
    outward, inward = lax.rem(row + 1, row_count), lax.rem(row + row_count - 1, row_count)

    layers = profile_ref.shape[0]
    gas = (0, layers, gas_out, gas_in, gas_twice)
    dust = (layers, planes - layers, dust_out, dust_in, dust_twice)
    loads = [
        pltpu.make_async_copy(source, target, load.at[n])
        for n, (source, target) in enumerate(
            ((mass_hbm, mass_ref), (phi_hbm, phi_ref), (rad_hbm, rad_ref), (tiles_hbm, tiles_ref))
        )
    ]
    for copy in loads:
        copy.start()

    barrier = pltpu.get_barrier_semaphore()

    def peer_of(step):
        near = step // 2
        return lax.rem(me + count // 2 + near * (2 * lax.rem(step, 2) - 1), count)

    @pl.loop(1, count)
    def _(step):
        pl.semaphore_signal(barrier, inc=1, device_id={"phi": lax.rem(me + step, count)}, device_id_type=MESH)

    pl.semaphore_signal(barrier, inc=1, device_id={"row": outward}, device_id_type=MESH)
    pl.semaphore_signal(barrier, inc=1, device_id={"row": inward}, device_id_type=MESH)

    def put_column(place, field, column):
        rows = [field[f].T[column : column + 1, :] for f in range(field.shape[0])]
        edge_out[place, : field.shape[0], :cells] = jnp.concatenate(rows, axis=0)

    def put_row(place, field, at):
        edge_out[place, : field.shape[0], :width] = field[:, at, :]

    def edge(place, target):
        return pltpu.make_async_remote_copy(
            src_ref=edge_out.at[place],
            dst_ref=edge_in.at[place],
            send_sem=edge_send.at[place],
            recv_sem=edge_recv.at[place],
            device_id=target,
            device_id_type=MESH,
        )

    def mass_edges(base, field):
        put_row(base, field, cells - 1)
        put_row(base + 1, field, 0)
        put_column(base + 2, field, width - 1)
        put_column(base + 3, field, 0)
        return [
            edge(base, {"phi": up}),
            edge(base + 1, {"phi": down}),
            edge(base + 2, {"row": outward}),
            edge(base + 3, {"row": inward}),
        ]

    def send_all(source, target, number):
        @pl.loop(1, count)
        def _(step):
            peer = peer_of(step)
            pltpu.make_async_remote_copy(
                src_ref=source.at[peer],
                dst_ref=target.at[me],
                send_sem=all_send.at[number],
                recv_sem=all_recv.at[number],
                device_id={"phi": peer},
                device_id_type=MESH,
            ).start()

        target[pl.ds(me, 1)] = source[pl.ds(me, 1)]

    def all_wait(target, semaphore):
        others = target.at[pl.ds(0, count - 1)]
        pltpu.make_async_copy(others, others, semaphore).wait()

    loads[0].wait()
    density = mass_ref[...]
    first_edges = mass_edges(0, density)
    loads[1].wait()
    loads[2].wait()
    put_row(12, phi_ref, 0)
    put_column(13, rad_ref, 0)
    first_edges += [edge(12, {"phi": down}), edge(13, {"row": inward})]
    names_in[pl.ds(me, 1)] = names_ref[...]

    pl.semaphore_wait(barrier, count + 1)
    for copy in first_edges:
        copy.start()

    @pl.loop(1, count)
    def _(step):
        pltpu.make_async_remote_copy(
            src_ref=names_ref.at[0],
            dst_ref=names_in.at[me],
            send_sem=all_send.at[0],
            recv_sem=all_recv.at[0],
            device_id={"phi": peer_of(step)},
            device_id_type=MESH,
        ).start()

    def send_tiles(number):
        for p in range(strip):
            tile_out[number, :, p, :] = fold(tiles_ref[number, :, p, :])
        send_all(tile_out.at[number], tile_in.at[number], 1 + number)

    loads[3].wait()

    lane = lax.broadcasted_iota(jnp.int32, (1, 1, width), 2)
    cell = lax.broadcasted_iota(jnp.int32, (1, cells, 1), 1)

    def rows_of(place, start, size):
        return edge_in[place, start : start + size, :width].reshape(size, 1, width)

    def columns_of(place, start, size, outside):
        turned = edge_in[place].T
        found = jnp.stack([turned[:cells, f : f + 1] for f in range(start, start + size)], axis=0)
        return jnp.where(outside, 0.0, found)

    for copy in first_edges:
        copy.wait()
    last_row = row == row_count - 1

    def advance(group, mass, base, start):
        first, size = group[:2]
        speed_phi, speed_rad = phi_ref[first : first + size], rad_ref[first : first + size]
        speed_next = jnp.where(cell == cells - 1, rows_of(12, first, size), pltpu.roll(speed_phi, cells - 1, 1))
        rim = columns_of(13, first, size, last_row)
        radial_next = jnp.where(lane == width - 1, rim, pltpu.roll(speed_rad, width - 1, 2))
        behind = jnp.where(cell == 0, rows_of(base, start, size), pltpu.roll(mass, 1, 1))
        ahead = jnp.where(cell == cells - 1, rows_of(base + 1, start, size), pltpu.roll(mass, cells - 1, 1))
        inner = jnp.where(lane == 0, columns_of(base + 2, start, size, row == 0), pltpu.roll(mass, 1, 2))
        rim = columns_of(base + 3, start, size, last_row)
        outer = jnp.where(lane == width - 1, rim, pltpu.roll(mass, width - 1, 2))
        flux_in = jnp.maximum(speed_phi, 0.0) * behind + jnp.minimum(speed_phi, 0.0) * mass
        flux_out = jnp.maximum(speed_next, 0.0) * mass + jnp.minimum(speed_next, 0.0) * ahead
        radial_in = jnp.maximum(speed_rad, 0.0) * inner + jnp.minimum(speed_rad, 0.0) * mass
        radial_out = jnp.maximum(radial_next, 0.0) * mass + jnp.minimum(radial_next, 0.0) * outer
        return mass - (flux_out - flux_in) - (radial_out - radial_in)

    def send_mass(group, mass, turn, channel):
        first, size, mass_out, mass_in, twice = group
        for f in range(size):
            mass_out[turn, :, f, :] = fold(mass[f])
        send_all(mass_out.at[turn], mass_in.at[turn], channel + turn)

    def make_deposit(number):
        line = lax.broadcasted_iota(jnp.int32, (lanes, lanes), 0)
        spot = lax.broadcasted_iota(jnp.int32, (lanes, lanes), 1)
        same = (line >= cells) == (spot >= cells)
        owner_line = lax.rem(line, cells).astype(jnp.float32)

        deposit[...] = jnp.zeros_like(deposit)

        @pl.loop(0, count // 2)
        def _(pair):
            for side in range(2):
                source = 2 * pair + side
                names = names_in[source]
                own, slot = names[2 * number : 2 * number + 1], names[2 * number + 1 : 2 * number + 2]
                block = tile_in[number, source]
                high = block.astype(jnp.bfloat16).astype(jnp.float32)
                left = block - high
                middle = left.astype(jnp.bfloat16).astype(jnp.float32)
                low = left - middle
                span = slice(side * lanes, (side + 1) * lanes)
                for n, part in enumerate((high, middle, low)):
                    spread = [jnp.where(slot == float(q), part, 0.0) for q in range(places)]
                    rhs[n * cells : (n + 1) * cells, span] = jnp.concatenate(spread, axis=0).astype(jnp.bfloat16)
                hit = jnp.where(same & (own == owner_line), 1.0, 0.0)
                lhs[:, span] = hit.astype(jnp.bfloat16)
            deposit[...] += lax.dot_general(
                lhs[...], rhs[...], (((1,), (1,)), ((), ())), preferred_element_type=jnp.float32
            )

        total = deposit[:, :cells] + deposit[:, cells : 2 * cells] + deposit[:, 2 * cells : 3 * cells]
        return jnp.concatenate([total[:count], total[cells : cells + count]], axis=1)

    spot = lax.broadcasted_iota(jnp.int32, (1, 1, lanes), 2)
    inside = lax.rem(spot, cells)

    def turn_back(group, number, added, turn, channel):
        first, size, mass_out, mass_in, twice = group
        all_wait(mass_in.at[turn - 1], all_recv.at[channel + turn - 1])
        for f in range(size):
            block = mass_in[turn - 1, :, f, :]
            if first + f < layers:
                block = block + profile_ref[first + f] * added
            twice[pl.ds(1, count), f, :] = block
            twice[pl.ds(1 + count, count), f, :] = block
            twice[0, f : f + 1, :] = block[count - 1 :]
        rest = rest_ref[number : number + 1].reshape(1, 1, lanes)
        low, high = whole_ref[number, 0], whole_ref[number, 1]
        here = jnp.where(spot < cells, twice[pl.ds(1 + count - low, count)], twice[pl.ds(1 + count - high, count)])
        prev = jnp.where(spot < cells, twice[pl.ds(count - low, count)], twice[pl.ds(count - high, count)])
        mixed = jnp.where(inside < cells - rest, here, prev)
        moved = inside - rest
        index = (spot - inside) + jnp.where(moved < 0, moved + cells, moved)
        index = jnp.broadcast_to(index, mixed.shape).reshape(count * size, lanes)
        mass_out[turn] = jnp.take_along_axis(mixed.reshape(count * size, lanes), index, axis=1).reshape(mixed.shape)
        send_all(mass_out.at[turn], mass_in.at[turn], channel + turn)

    def regain(group, turn, channel, target, start):
        first, size, mass_out, mass_in, twice = group
        all_wait(mass_in.at[turn], all_recv.at[channel + turn])
        for f in range(size):
            target[start + f] = unfold(mass_in[turn, :, f, :])

    def begin_edges(group, base):
        first, size = group[:2]
        copies = mass_edges(base, held_mass[first : first + size])
        for copy in copies:
            copy.start()
        return copies

    def second(group, copies, base, channel):
        first, size = group[:2]
        for copy in copies:
            copy.wait()
        send_mass(group, advance(group, held_mass[first : first + size], base, 0), 2, channel)

    def first_half(group, channel):
        first, size = group[:2]
        send_mass(group, advance(group, mass_ref[first : first + size], 0, first), 0, channel)

    first_half(dust, 3)
    send_tiles(0)
    first_half(gas, 7)
    turn_back(dust, 0, None, 1, 3)
    all_wait(names_in, all_recv.at[0])
    all_wait(tile_in.at[0], all_recv.at[1])
    added = make_deposit(0)
    turn_back(gas, 0, added, 1, 7)
    send_tiles(1)
    regain(dust, 1, 3, held_mass, dust[0])
    dust_edges = begin_edges(dust, 4)
    regain(gas, 1, 7, held_mass, gas[0])
    gas_edges = begin_edges(gas, 8)
    second(dust, dust_edges, 4, 3)
    second(gas, gas_edges, 8, 7)
    all_wait(tile_in.at[1], all_recv.at[2])
    added = make_deposit(1)
    turn_back(dust, 1, None, 3, 3)
    turn_back(gas, 1, added, 3, 7)
    regain(dust, 3, 3, out_ref, dust[0])
    regain(gas, 3, 7, out_ref, gas[0])
    all_wait(names_in, all_send.at[0])
    for number in range(steps):
        all_wait(tile_out.at[number], all_send.at[1 + number])
    for group, channel in ((dust, 3), (gas, 7)):
        for turn in range(4):
            all_wait(group[2].at[turn], all_send.at[channel + turn])


def body(density, phi_speed, rad_speed, profile, tiles, owners, slots, shifts):
    fluids, layers, cells, width = density.shape
    planes = fluids * layers
    count = lax.axis_size("phi")
    per = width // count
    steps, held, strip = tiles.shape[:3]
    lanes = per * cells
    me = lax.axis_index("phi")
    shape = (planes, cells, width)
    mine = lax.dynamic_slice_in_dim(shifts.reshape(steps, per, count), me, 1, axis=2)[:, :, 0]
    whole = mine // cells
    rest = jnp.repeat(mine % cells, cells, axis=1)
    names = jnp.stack([owners[:, :, 0], slots], axis=1).astype(jnp.float32)
    names = jnp.tile(names, (1, 1, per)).reshape(1, 2 * steps, lanes)
    smem, vmem = pl.BlockSpec(memory_space=pltpu.SMEM), pl.BlockSpec(memory_space=pltpu.VMEM)
    sent = 4 * count * lanes * (4 * planes + 2 * strip + 4)
    out = pl.pallas_call(
        fused,
        out_shape=jax.ShapeDtypeStruct(shape, jnp.float32),
        in_specs=[smem] * 2 + [vmem] * 2 + [pl.BlockSpec(memory_space=pltpu.HBM)] * 4,
        out_specs=vmem,
        scratch_shapes=[
            pltpu.VMEM(shape, jnp.float32),
            pltpu.VMEM(shape, jnp.float32),
            pltpu.VMEM(shape, jnp.float32),
            pltpu.VMEM(tiles.shape, jnp.float32),
            pltpu.VMEM((14, 8, 128), jnp.float32),
            pltpu.VMEM((14, 8, 128), jnp.float32),
            pltpu.VMEM((count, 2 * steps, lanes), jnp.float32),
            pltpu.VMEM((steps, count, strip, lanes), jnp.float32),
            pltpu.VMEM((steps, count, strip, lanes), jnp.float32),
            pltpu.VMEM((4, count, layers, lanes), jnp.float32),
            pltpu.VMEM((4, count, layers, lanes), jnp.float32),
            pltpu.VMEM((2 * count + 1, layers, lanes), jnp.float32),
            pltpu.VMEM((4, count, planes - layers, lanes), jnp.float32),
            pltpu.VMEM((4, count, planes - layers, lanes), jnp.float32),
            pltpu.VMEM((2 * count + 1, planes - layers, lanes), jnp.float32),
            pltpu.VMEM(shape, jnp.float32),
            pltpu.VMEM((lanes, 2 * lanes), jnp.bfloat16),
            pltpu.VMEM((3 * cells, 2 * lanes), jnp.bfloat16),
            pltpu.VMEM((lanes, 3 * cells), jnp.float32),
            pltpu.SemaphoreType.DMA((14,)),
            pltpu.SemaphoreType.DMA((14,)),
            pltpu.SemaphoreType.DMA((11,)),
            pltpu.SemaphoreType.DMA((11,)),
            pltpu.SemaphoreType.DMA((4,)),
        ],
        compiler_params=pltpu.CompilerParams(
            collective_id=0, has_side_effects=True, vmem_limit_bytes=67043328
        ),
        cost_estimate=pl.CostEstimate(flops=10**9, bytes_accessed=sent, transcendentals=0),
    )(
        whole,
        profile,
        rest,
        names,
        density.reshape(shape),
        phi_speed.reshape(shape),
        rad_speed.reshape(shape),
        tiles,
    )
    return out.reshape(density.shape)


def solution(mesh):
    placed = (
        P(None, None, "phi", "row"),
        P(None, None, "phi", "row"),
        P(None, None, "phi", "row"),
        P(),
        P(None, "phi", None, "row"),
        P(None, "phi", None),
        P(None, "phi"),
        P(None, "row"),
    )
    return jax.shard_map(
        body, mesh=mesh, in_specs=placed, out_specs=P(None, None, "phi", "row"), check_vma=False
    )
```

```python
import jax
import jax.numpy as jnp
from jax import lax
from jax.experimental import pallas as pl
from jax.experimental.pallas import tpu as pltpu
from jax.sharding import PartitionSpec as P

MESH = pl.DeviceIdType.MESH


def fold(block):
    turned = block.T
    count = turned.shape[0] // 2
    return jnp.concatenate([turned[:count], turned[count:]], axis=1)


def unfold(block):
    half = block.shape[1] // 2
    return jnp.concatenate([block[:, :half], block[:, half:]], axis=0).T


def fused(
    whole_ref,
    profile_ref,
    rest_ref,
    names_ref,
    mass_hbm,
    phi_hbm,
    rad_hbm,
    tiles_hbm,
    out_ref,
    mass_ref,
    phi_ref,
    rad_ref,
    tiles_ref,
    edge_out,
    edge_in,
    names_in,
    tile_out,
    tile_in,
    gas_out,
    gas_in,
    gas_twice,
    dust_out,
    dust_in,
    dust_twice,
    held_mass,
    lhs,
    rhs,
    deposit,
    edge_send,
    edge_recv,
    all_send,
    all_recv,
    load,
):
    planes, cells, width = mass_ref.shape
    steps = tiles_ref.shape[0]
    strip = tiles_ref.shape[2]
    places = cells // strip
    count, row_count = lax.axis_size("phi"), lax.axis_size("row")
    me, row = lax.axis_index("phi"), lax.axis_index("row")
    lanes = 2 * cells
    up, down = lax.rem(me + 1, count), lax.rem(me + count - 1, count)
    outward, inward = lax.rem(row + 1, row_count), lax.rem(row + row_count - 1, row_count)

    layers = profile_ref.shape[0]
    gas = (0, layers, gas_out, gas_in, gas_twice)
    dust = (layers, planes - layers, dust_out, dust_in, dust_twice)
    loads = [
        pltpu.make_async_copy(source, target, load.at[n])
        for n, (source, target) in enumerate(
            ((mass_hbm, mass_ref), (phi_hbm, phi_ref), (rad_hbm, rad_ref), (tiles_hbm, tiles_ref))
        )
    ]
    for copy in loads:
        copy.start()

    barrier = pltpu.get_barrier_semaphore()

    def peer_of(step):
        near = step // 2
        return lax.rem(me + count // 2 + near * (2 * lax.rem(step, 2) - 1), count)

    @pl.loop(1, count)
    def _(step):
        pl.semaphore_signal(barrier, inc=1, device_id={"phi": lax.rem(me + step, count)}, device_id_type=MESH)

    pl.semaphore_signal(barrier, inc=1, device_id={"row": outward}, device_id_type=MESH)
    pl.semaphore_signal(barrier, inc=1, device_id={"row": inward}, device_id_type=MESH)

    def put_column(place, field, column):
        rows = [field[f].T[column : column + 1, :] for f in range(field.shape[0])]
        edge_out[place, : field.shape[0], :cells] = jnp.concatenate(rows, axis=0)

    def put_row(place, field, at):
        edge_out[place, : field.shape[0], :width] = field[:, at, :]

    def edge(place, target):
        return pltpu.make_async_remote_copy(
            src_ref=edge_out.at[place],
            dst_ref=edge_in.at[place],
            send_sem=edge_send.at[place],
            recv_sem=edge_recv.at[place],
            device_id=target,
            device_id_type=MESH,
        )

    def mass_edges(base, field):
        put_row(base, field, cells - 1)
        put_row(base + 1, field, 0)
        put_column(base + 2, field, width - 1)
        put_column(base + 3, field, 0)
        return [
            edge(base, {"phi": up}),
            edge(base + 1, {"phi": down}),
            edge(base + 2, {"row": outward}),
            edge(base + 3, {"row": inward}),
        ]

    def send_all(source, target, number):
        @pl.loop(1, count)
        def _(step):
            peer = peer_of(step)
            pltpu.make_async_remote_copy(
                src_ref=source.at[peer],
                dst_ref=target.at[me],
                send_sem=all_send.at[number],
                recv_sem=all_recv.at[number],
                device_id={"phi": peer},
                device_id_type=MESH,
            ).start()

        target[pl.ds(me, 1)] = source[pl.ds(me, 1)]

    def all_wait(target, semaphore):
        others = target.at[pl.ds(0, count - 1)]
        pltpu.make_async_copy(others, others, semaphore).wait()

    loads[0].wait()
    density = mass_ref[...]
    first_edges = mass_edges(0, density)
    loads[1].wait()
    loads[2].wait()
    put_row(12, phi_ref, 0)
    put_column(13, rad_ref, 0)
    first_edges += [edge(12, {"phi": down}), edge(13, {"row": inward})]
    names_in[pl.ds(me, 1)] = names_ref[...]

    pl.semaphore_wait(barrier, count + 1)
    for copy in first_edges:
        copy.start()

    @pl.loop(1, count)
    def _(step):
        pltpu.make_async_remote_copy(
            src_ref=names_ref.at[0],
            dst_ref=names_in.at[me],
            send_sem=all_send.at[0],
            recv_sem=all_recv.at[0],
            device_id={"phi": peer_of(step)},
            device_id_type=MESH,
        ).start()

    def send_tiles(number):
        for p in range(strip):
            tile_out[number, :, p, :] = fold(tiles_ref[number, :, p, :])
        send_all(tile_out.at[number], tile_in.at[number], 1 + number)

    loads[3].wait()

    lane = lax.broadcasted_iota(jnp.int32, (1, 1, width), 2)
    cell = lax.broadcasted_iota(jnp.int32, (1, cells, 1), 1)

    def rows_of(place, start, size):
        return edge_in[place, start : start + size, :width].reshape(size, 1, width)

    def columns_of(place, start, size, outside):
        turned = edge_in[place].T
        found = jnp.stack([turned[:cells, f : f + 1] for f in range(start, start + size)], axis=0)
        return jnp.where(outside, 0.0, found)

    for copy in first_edges:
        copy.wait()
    last_row = row == row_count - 1

    def advance(group, mass, base, start):
        first, size = group[:2]
        speed_phi, speed_rad = phi_ref[first : first + size], rad_ref[first : first + size]
        speed_next = jnp.where(cell == cells - 1, rows_of(12, first, size), pltpu.roll(speed_phi, cells - 1, 1))
        rim = columns_of(13, first, size, last_row)
        radial_next = jnp.where(lane == width - 1, rim, pltpu.roll(speed_rad, width - 1, 2))
        behind = jnp.where(cell == 0, rows_of(base, start, size), pltpu.roll(mass, 1, 1))
        ahead = jnp.where(cell == cells - 1, rows_of(base + 1, start, size), pltpu.roll(mass, cells - 1, 1))
        inner = jnp.where(lane == 0, columns_of(base + 2, start, size, row == 0), pltpu.roll(mass, 1, 2))
        rim = columns_of(base + 3, start, size, last_row)
        outer = jnp.where(lane == width - 1, rim, pltpu.roll(mass, width - 1, 2))
        flux_in = jnp.maximum(speed_phi, 0.0) * behind + jnp.minimum(speed_phi, 0.0) * mass
        flux_out = jnp.maximum(speed_next, 0.0) * mass + jnp.minimum(speed_next, 0.0) * ahead
        radial_in = jnp.maximum(speed_rad, 0.0) * inner + jnp.minimum(speed_rad, 0.0) * mass
        radial_out = jnp.maximum(radial_next, 0.0) * mass + jnp.minimum(radial_next, 0.0) * outer
        return mass - (flux_out - flux_in) - (radial_out - radial_in)

    def send_mass(group, mass, turn, channel):
        first, size, mass_out, mass_in, twice = group
        for f in range(size):
            mass_out[turn, :, f, :] = fold(mass[f])
        send_all(mass_out.at[turn], mass_in.at[turn], channel + turn)

    def make_deposit(number):
        line = lax.broadcasted_iota(jnp.int32, (lanes, lanes), 0)
        spot = lax.broadcasted_iota(jnp.int32, (lanes, lanes), 1)
        same = (line >= cells) == (spot >= cells)
        owner_line = lax.rem(line, cells).astype(jnp.float32)

        deposit[...] = jnp.zeros_like(deposit)

        @pl.loop(0, count // 2)
        def _(pair):
            for side in range(2):
                source = 2 * pair + side
                name = names_in[source][:, number * cells : (number + 1) * cells]
                name = jnp.concatenate([name, name], axis=1)
                own = jnp.floor(name * (1.0 / places))
                slot = name - own * places
                block = tile_in[number, source]
                high = block.astype(jnp.bfloat16).astype(jnp.float32)
                left = block - high
                middle = left.astype(jnp.bfloat16).astype(jnp.float32)
                low = left - middle
                span = slice(side * lanes, (side + 1) * lanes)
                for n, part in enumerate((high, middle, low)):
                    spread = [jnp.where(slot == float(q), part, 0.0) for q in range(places)]
                    rhs[n * cells : (n + 1) * cells, span] = jnp.concatenate(spread, axis=0).astype(jnp.bfloat16)
                hit = jnp.where(same & (own == owner_line), 1.0, 0.0)
                lhs[:, span] = hit.astype(jnp.bfloat16)
            deposit[...] += lax.dot_general(
                lhs[...], rhs[...], (((1,), (1,)), ((), ())), preferred_element_type=jnp.float32
            )

        total = deposit[:, :cells] + deposit[:, cells : 2 * cells] + deposit[:, 2 * cells : 3 * cells]
        return jnp.concatenate([total[:count], total[cells : cells + count]], axis=1)

    spot = lax.broadcasted_iota(jnp.int32, (1, 1, lanes), 2)
    inside = lax.rem(spot, cells)

    def turn_back(group, number, added, turn, channel):
        first, size, mass_out, mass_in, twice = group
        all_wait(mass_in.at[turn - 1], all_recv.at[channel + turn - 1])
        for f in range(size):
            block = mass_in[turn - 1, :, f, :]
            if first + f < layers:
                block = block + profile_ref[first + f] * added
            twice[pl.ds(1, count), f, :] = block
            twice[pl.ds(1 + count, count), f, :] = block
            twice[0, f : f + 1, :] = block[count - 1 :]
        rest = rest_ref[number : number + 1].reshape(1, 1, lanes)
        low, high = whole_ref[number, 0], whole_ref[number, 1]
        here = jnp.where(spot < cells, twice[pl.ds(1 + count - low, count)], twice[pl.ds(1 + count - high, count)])
        prev = jnp.where(spot < cells, twice[pl.ds(count - low, count)], twice[pl.ds(count - high, count)])
        mixed = jnp.where(inside < cells - rest, here, prev)
        moved = inside - rest
        index = (spot - inside) + jnp.where(moved < 0, moved + cells, moved)
        index = jnp.broadcast_to(index, mixed.shape).reshape(count * size, lanes)
        mass_out[turn] = jnp.take_along_axis(mixed.reshape(count * size, lanes), index, axis=1).reshape(mixed.shape)
        send_all(mass_out.at[turn], mass_in.at[turn], channel + turn)

    def regain(group, turn, channel, target, start):
        first, size, mass_out, mass_in, twice = group
        all_wait(mass_in.at[turn], all_recv.at[channel + turn])
        for f in range(size):
            target[start + f] = unfold(mass_in[turn, :, f, :])

    def begin_edges(group, base):
        first, size = group[:2]
        copies = mass_edges(base, held_mass[first : first + size])
        for copy in copies:
            copy.start()
        return copies

    def second(group, copies, base, channel):
        first, size = group[:2]
        for copy in copies:
            copy.wait()
        send_mass(group, advance(group, held_mass[first : first + size], base, 0), 2, channel)

    def first_half(group, channel):
        first, size = group[:2]
        send_mass(group, advance(group, mass_ref[first : first + size], 0, first), 0, channel)

    first_half(dust, 3)
    send_tiles(0)
    first_half(gas, 7)
    turn_back(dust, 0, None, 1, 3)
    all_wait(names_in, all_recv.at[0])
    all_wait(tile_in.at[0], all_recv.at[1])
    added = make_deposit(0)
    turn_back(gas, 0, added, 1, 7)
    send_tiles(1)
    regain(dust, 1, 3, held_mass, dust[0])
    dust_edges = begin_edges(dust, 4)
    regain(gas, 1, 7, held_mass, gas[0])
    gas_edges = begin_edges(gas, 8)
    second(dust, dust_edges, 4, 3)
    second(gas, gas_edges, 8, 7)
    all_wait(tile_in.at[1], all_recv.at[2])
    added = make_deposit(1)
    turn_back(dust, 1, None, 3, 3)
    turn_back(gas, 1, added, 3, 7)
    regain(dust, 3, 3, out_ref, dust[0])
    regain(gas, 3, 7, out_ref, gas[0])
    all_wait(names_in, all_send.at[0])
    for number in range(steps):
        all_wait(tile_out.at[number], all_send.at[1 + number])
    for group, channel in ((dust, 3), (gas, 7)):
        for turn in range(4):
            all_wait(group[2].at[turn], all_send.at[channel + turn])


def body(density, phi_speed, rad_speed, profile, tiles, owners, slots, shifts):
    fluids, layers, cells, width = density.shape
    planes = fluids * layers
    count = lax.axis_size("phi")
    per = width // count
    steps, held, strip = tiles.shape[:3]
    lanes = per * cells
    me = lax.axis_index("phi")
    shape = (planes, cells, width)
    mine = lax.dynamic_slice_in_dim(shifts.reshape(steps, per, count), me, 1, axis=2)[:, :, 0]
    whole = mine // cells
    rest = jnp.repeat(mine % cells, cells, axis=1)
    names = (owners[:, :, 0] * (cells // strip) + slots).astype(jnp.float32).reshape(1, 1, lanes)
    smem, vmem = pl.BlockSpec(memory_space=pltpu.SMEM), pl.BlockSpec(memory_space=pltpu.VMEM)
    sent = 4 * count * lanes * (4 * planes + 2 * strip + 1)
    out = pl.pallas_call(
        fused,
        out_shape=jax.ShapeDtypeStruct(shape, jnp.float32),
        in_specs=[smem] * 2 + [vmem] * 2 + [pl.BlockSpec(memory_space=pltpu.HBM)] * 4,
        out_specs=vmem,
        scratch_shapes=[
            pltpu.VMEM(shape, jnp.float32),
            pltpu.VMEM(shape, jnp.float32),
            pltpu.VMEM(shape, jnp.float32),
            pltpu.VMEM(tiles.shape, jnp.float32),
            pltpu.VMEM((14, 8, 128), jnp.float32),
            pltpu.VMEM((14, 8, 128), jnp.float32),
            pltpu.VMEM((count, 1, lanes), jnp.float32),
            pltpu.VMEM((steps, count, strip, lanes), jnp.float32),
            pltpu.VMEM((steps, count, strip, lanes), jnp.float32),
            pltpu.VMEM((4, count, layers, lanes), jnp.float32),
            pltpu.VMEM((4, count, layers, lanes), jnp.float32),
            pltpu.VMEM((2 * count + 1, layers, lanes), jnp.float32),
            pltpu.VMEM((4, count, planes - layers, lanes), jnp.float32),
            pltpu.VMEM((4, count, planes - layers, lanes), jnp.float32),
            pltpu.VMEM((2 * count + 1, planes - layers, lanes), jnp.float32),
            pltpu.VMEM(shape, jnp.float32),
            pltpu.VMEM((lanes, 2 * lanes), jnp.bfloat16),
            pltpu.VMEM((3 * cells, 2 * lanes), jnp.bfloat16),
            pltpu.VMEM((lanes, 3 * cells), jnp.float32),
            pltpu.SemaphoreType.DMA((14,)),
            pltpu.SemaphoreType.DMA((14,)),
            pltpu.SemaphoreType.DMA((11,)),
            pltpu.SemaphoreType.DMA((11,)),
            pltpu.SemaphoreType.DMA((4,)),
        ],
        compiler_params=pltpu.CompilerParams(
            collective_id=0, has_side_effects=True, vmem_limit_bytes=67043328
        ),
        cost_estimate=pl.CostEstimate(flops=10**9, bytes_accessed=sent, transcendentals=0),
    )(
        whole,
        profile,
        rest,
        names,
        density.reshape(shape),
        phi_speed.reshape(shape),
        rad_speed.reshape(shape),
        tiles,
    )
    return out.reshape(density.shape)


def solution(mesh):
    placed = (
        P(None, None, "phi", "row"),
        P(None, None, "phi", "row"),
        P(None, None, "phi", "row"),
        P(),
        P(None, "phi", None, "row"),
        P(None, "phi", None),
        P(None, "phi"),
        P(None, "row"),
    )
    return jax.shard_map(
        body, mesh=mesh, in_specs=placed, out_specs=P(None, None, "phi", "row"), check_vma=False
    )
```
